32 devices in a mesh: grp: 2 (over y), seq: 4 (over z), head: 2 (over x), sub: 2 (over core).
Axes of the slice: x: 2, y: 2, z: 4, core: 2. Of those that a mesh axis runs over, the one named last changes fastest.
Arguments:
- queries: bfloat16 [768, 5120], P(('grp', 'seq', 'head', 'sub')), parts along dimension 0, may hold values from -24 to 24
- keys: bfloat16 [768, 5120], P(('grp', 'seq', 'head', 'sub')), parts along dimension 0, may hold values from -24 to 24
- values: bfloat16 [768, 5120], P(('grp', 'seq', 'head', 'sub')), parts along dimension 0, may hold values from -6 to 6
- q_gain: float32 [5120], replicated, may hold values from 0.5 to 4
- k_gain: float32 [5120], replicated, may hold values from 0.5 to 4
Outputs:
- attended: bfloat16 [768, 5120], P(('grp', 'seq', 'head', 'sub')), parts along dimension 0
The draws below stay inside these ranges and needn't reach their ends.
There are 2 independent parts, one for each index of `grp`. The reference program is written for one: setup_inputs(seed, part) draws one part's arguments, and reference() takes and returns one part's arrays. A program takes and returns all parts, laid end to end along the dimension named above; an argument that names none is the same for every part. Nothing has to cross between parts.
All inputs are finite; a program needn't handle non-finite values.
Results may differ from the reference program's by a relative error of at most 0.012.
The reference program's roundings to bfloat16 on the way (of `q_normed`, `k_normed` and `probs`) count: a program that leaves them out, or rounds other values in their place, can miss the bound.
Values may be sent and summed in bfloat16 or wider, within the bound.
No kernel may reach another device: no remote copies, remote signals or barrier semaphores. Data moves between devices by JAX's collectives and lax.ppermute only.
A program may use at most 64 MiB of HBM per device.

```python
import math
import jax
import jax.numpy as jnp
from jax import lax

H = 40
HD = 128
TOKENS = 384
WIDTH = 5120


def base_matrix(key, which):
    source = jax.random.fold_in(key, 40 + which)
    return jnp.clip(jax.random.normal(source, (TOKENS, H * HD), jnp.float32), -6.0, 6.0)


def draw_queries(key, part):
    matrix = base_matrix(key, 0)
    return matrix.astype(jnp.bfloat16)


def draw_keys(key, part):
    matrix = base_matrix(key, 1)
    return matrix.astype(jnp.bfloat16)


def block_scale(own_key, extent, shards, least, high):
    def one(dim, blocks):
        steps = jax.random.uniform(jax.random.fold_in(jax.random.fold_in(own_key, 6), dim), (blocks,), jnp.float32, least / len(shards), high / len(shards))
        return jnp.repeat(jnp.exp(steps), extent[dim] // blocks).reshape((-1,) + (1,) * (len(extent) - dim - 1))

    loudness = one(*shards[0])
    for cut in shards[1:]:
        loudness = loudness * one(*cut)
    return loudness


def gaussian(own_key, extent, spread, limit, shards=(), dtype=jnp.bfloat16):
    level = block_scale(own_key, extent, shards, -0.22, 0.18) if shards else 1.0
    values = jax.random.normal(own_key, extent, jnp.float32) * spread * level
    return jnp.minimum(jnp.maximum(values, -limit), limit).astype(dtype)


def setup_inputs(seed: int = 0, part: int = 0) -> dict:
    streams_of = jax.random.split(jax.random.key(seed), 6)
    part_splits = jax.random.split(jax.random.fold_in(streams_of[5], part), 6)
    queries = draw_queries(jax.random.fold_in(jax.random.fold_in(streams_of[5], part), 71), part)
    keys = draw_keys(jax.random.fold_in(jax.random.fold_in(streams_of[5], part), 71), part)
    values = gaussian(part_splits[2], (TOKENS, WIDTH), 1.0, 6.0, ((0, 16),))
    q_gain = jnp.clip(jnp.exp(jax.random.uniform(streams_of[3], (WIDTH,), jnp.float32, math.log(0.5), math.log(4.0))), 0.5, 4.0)
    k_gain = jnp.clip(jnp.exp(jax.random.uniform(streams_of[4], (WIDTH,), jnp.float32, math.log(0.5), math.log(4.0))), 0.5, 4.0)
    return {"queries": queries, "keys": keys, "values": values, "q_gain": q_gain, "k_gain": k_gain}


EPS = 1e-06

def normalize(matrix, gain):
    widened = matrix.astype(jnp.float32)
    inverse = lax.rsqrt(lax.optimization_barrier(jnp.mean(widened * widened, axis=-1, keepdims=True)) + EPS)
    return (widened * inverse * gain).astype(jnp.bfloat16)

def reference(queries, keys, values, q_gain, k_gain):
    q_normed = normalize(queries, q_gain)
    k_normed = normalize(keys, k_gain)
    q_heads = q_normed.reshape(TOKENS, H, HD).transpose(1, 0, 2)
    k_heads = k_normed.reshape(TOKENS, H, HD).transpose(1, 0, 2)
    v_heads = values.reshape(TOKENS, H, HD).transpose(1, 0, 2)
    block_size = math.gcd(TOKENS, 1024)
    factor = 1.0 / math.sqrt(HD)

    def one_head(triple):
        q_head, k_head, v_head = triple
        q_blocks = q_head.reshape(TOKENS // block_size, block_size, HD)

        def one_block(q_block):
            scores = jnp.dot(q_block, k_head.T, preferred_element_type=jnp.float32) * factor
            highest = lax.optimization_barrier(jnp.max(scores, axis=-1, keepdims=True))
            weights = jnp.exp(scores - highest)
            weight_sum = lax.optimization_barrier(jnp.sum(weights, axis=-1, keepdims=True))
            probs = weights.astype(jnp.bfloat16)
            weighted = jnp.dot(probs, v_head, preferred_element_type=jnp.float32)
            return (weighted / weight_sum).astype(jnp.bfloat16)
        return lax.map(one_block, q_blocks).reshape(TOKENS, HD)
    outputs = lax.map(one_head, (q_heads, k_heads, v_heads))
    return outputs.transpose(1, 0, 2).reshape(TOKENS, H * HD)
```

```python
import functools
import math

import jax
import jax.numpy as jnp
from jax import lax
from jax.experimental import pallas as pl
from jax.experimental.pallas import tpu as pltpu
from jax.sharding import PartitionSpec as P

HD = 128


EPS = 1e-06


def normalize(matrix, gain):
    widened = matrix.astype(jnp.float32)
    inverse = lax.rsqrt(jnp.mean(widened * widened, axis=-1, keepdims=True) + EPS)
    return (widened * inverse * gain).astype(jnp.bfloat16)


def gathered_body(queries, keys, values, q_gain, k_gain):
    q_normed = normalize(queries, q_gain)
    k_normed = normalize(keys, k_gain)
    q_local, k_local, v_local = (
        lax.all_to_all(q_normed, "head", split_axis=1, concat_axis=0, tiled=True),
        lax.all_to_all(k_normed, "head", split_axis=1, concat_axis=0, tiled=True),
        lax.all_to_all(values, "head", split_axis=1, concat_axis=0, tiled=True),
    )
    query_count = q_local.shape[0]
    local_heads = q_local.shape[1] // HD
    factor = 1.0 / math.sqrt(HD)
    q_heads = q_local.reshape(query_count, local_heads, HD).transpose(1, 0, 2)
    initial = (
        jnp.full((local_heads, query_count), -1e30, jnp.float32),
        jnp.zeros((local_heads, query_count), jnp.float32),
        jnp.zeros((local_heads, query_count, HD), jnp.float32),
    )
    half_rows = q_local.shape[0]
    key_piece = lax.all_gather(k_local, ("seq", "sub"), axis=0, tiled=True)
    value_piece = lax.all_gather(v_local, ("seq", "sub"), axis=0, tiled=True)
    row_count = key_piece.shape[0]
    block_size = math.gcd(row_count, 512)
    turn_count = row_count // block_size
    key_blocks = key_piece.reshape(turn_count, block_size, local_heads, HD)
    value_blocks = value_piece.reshape(turn_count, block_size, local_heads, HD)

    def advance(state, block_pair):
        key_block, value_block = block_pair
        highest, weight_sum, weighted = state
        scores = (
            jnp.einsum("hqd,khd->hqk", q_heads, key_block, preferred_element_type=jnp.float32)
            * factor
        )
        new_high = jnp.maximum(highest, jnp.max(scores, axis=-1))
        shrink = jnp.exp(highest - new_high)
        weights = jnp.exp(scores - new_high[..., None])
        new_sum = weight_sum * shrink + jnp.sum(weights, axis=-1)
        probs = weights.astype(jnp.bfloat16)
        added = jnp.einsum("hqk,khd->hqd", probs, value_block, preferred_element_type=jnp.float32)
        return ((new_high, new_sum, weighted * shrink[..., None] + added), None)

    partial_value = lax.scan(advance, initial, (key_blocks, value_blocks))[0]
    weight_sum = partial_value[1]
    weighted = partial_value[2]
    result = weighted / weight_sum[..., None]
    outputs = result.transpose(1, 0, 2).reshape(half_rows, local_heads * HD).astype(jnp.bfloat16)
    return lax.all_to_all(outputs, "head", split_axis=0, concat_axis=1, tiled=True)


CHIP = ("seq", "head")


def pack_kernel(chips, q_ref, k_ref, v_ref, qg_ref, kg_ref, out_ref):
    rows, width = q_ref.shape
    part = width // chips
    q_normed = normalize(q_ref[...], qg_ref[...])
    k_normed = normalize(k_ref[...], kg_ref[...])
    for chip in range(chips):
        columns = slice(chip * part, (chip + 1) * part)
        out_ref[chip, 0:rows, :] = v_ref[:, columns]
        out_ref[chip, rows : 2 * rows, :] = k_normed[:, columns]
        out_ref[chip, 2 * rows : 3 * rows, :] = q_normed[:, columns]


def attend_kernel(chips, rows, mine_ref, other_ref, out_ref):
    heads = mine_ref.shape[2] // HD
    factor = 1.0 / math.sqrt(HD)

    def joined(refs, first, columns):
        pieces = [
            ref[chip, first : first + rows, columns].astype(jnp.float32)
            for ref in refs
            for chip in range(chips)
        ]
        return jnp.concatenate(pieces, axis=0).astype(jnp.bfloat16)

    for head in range(heads):
        columns = slice(head * HD, (head + 1) * HD)
        v_head = joined((mine_ref, other_ref), 0, columns)
        k_head = joined((mine_ref, other_ref), rows, columns)
        q_head = joined((mine_ref,), 2 * rows, columns)
        scores = (
            lax.dot_general(
                q_head, k_head, (((1,), (1,)), ((), ())), preferred_element_type=jnp.float32
            )
            * factor
        )
        highest = jnp.max(scores, axis=-1, keepdims=True)
        weights = jnp.exp(scores - highest)
        weight_sum = jnp.sum(weights, axis=-1, keepdims=True)
        weighted = jnp.dot(weights.astype(jnp.bfloat16), v_head, preferred_element_type=jnp.float32)
        result = (weighted / weight_sum).astype(jnp.bfloat16)
        for chip in range(chips):
            out_ref[chip, :, columns] = result[chip * rows : (chip + 1) * rows, :]


def split_body(chips, queries, keys, values, q_gain, k_gain):
    rows, width = queries.shape
    part = width // chips
    packed = pl.pallas_call(
        functools.partial(pack_kernel, chips),
        out_shape=jax.ShapeDtypeStruct((chips, 3 * rows, part), jnp.bfloat16),
    )(queries, keys, values, q_gain[None, :], k_gain[None, :])
    mine = lax.all_to_all(packed, CHIP, split_axis=0, concat_axis=0, tiled=True)
    swap = [(0, 1), (1, 0)]
    other = lax.ppermute(mine[:, : 2 * rows], "sub", swap)
    attended = pl.pallas_call(
        functools.partial(attend_kernel, chips, rows),
        out_shape=jax.ShapeDtypeStruct((chips, rows, part), jnp.bfloat16),
    )(mine, other)
    back = lax.all_to_all(attended, CHIP, split_axis=0, concat_axis=0, tiled=True)
    return back.transpose(1, 0, 2).reshape(rows, width)


def solution(mesh):
    chips = mesh.shape["seq"] * mesh.shape["head"]

    def body(queries, *rest):
        heads = queries.shape[1] // HD
        if heads % chips or mesh.shape["sub"] != 2:
            return gathered_body(queries, *rest)
        return split_body(chips, queries, *rest)

    token_spec = P(("grp", "seq", "head", "sub"), None)
    in_specs = (token_spec, token_spec, token_spec, P(), P())
    return jax.shard_map(
        body, mesh=mesh, in_specs=in_specs, out_specs=token_spec, check_vma=False
    )
```

```python
import functools
import math

import jax
import jax.numpy as jnp
from jax import lax
from jax.experimental import pallas as pl
from jax.experimental.pallas import tpu as pltpu
from jax.sharding import PartitionSpec as P


HD = 128


EPS = 1e-06


def normalize(matrix, gain):
    widened = matrix.astype(jnp.float32)
    inverse = lax.rsqrt(jnp.mean(widened * widened, axis=-1, keepdims=True) + EPS)
    return (widened * inverse * gain).astype(jnp.bfloat16)


def gathered_body(queries, keys, values, q_gain, k_gain):
    q_normed = normalize(queries, q_gain)
    k_normed = normalize(keys, k_gain)
    q_local, k_local, v_local = (
        lax.all_to_all(q_normed, "head", split_axis=1, concat_axis=0, tiled=True),
        lax.all_to_all(k_normed, "head", split_axis=1, concat_axis=0, tiled=True),
        lax.all_to_all(values, "head", split_axis=1, concat_axis=0, tiled=True),
    )
    query_count = q_local.shape[0]
    local_heads = q_local.shape[1] // HD
    factor = 1.0 / math.sqrt(HD)
    q_heads = q_local.reshape(query_count, local_heads, HD).transpose(1, 0, 2)
    initial = (
        jnp.full((local_heads, query_count), -1e30, jnp.float32),
        jnp.zeros((local_heads, query_count), jnp.float32),
        jnp.zeros((local_heads, query_count, HD), jnp.float32),
    )
    half_rows = q_local.shape[0]
    key_piece = lax.all_gather(k_local, ("seq", "sub"), axis=0, tiled=True)
    value_piece = lax.all_gather(v_local, ("seq", "sub"), axis=0, tiled=True)
    row_count = key_piece.shape[0]
    block_size = math.gcd(row_count, 512)
    turn_count = row_count // block_size
    key_blocks = key_piece.reshape(turn_count, block_size, local_heads, HD)
    value_blocks = value_piece.reshape(turn_count, block_size, local_heads, HD)

    def advance(state, block_pair):
        key_block, value_block = block_pair
        highest, weight_sum, weighted = state
        scores = (
            jnp.einsum("hqd,khd->hqk", q_heads, key_block, preferred_element_type=jnp.float32)
            * factor
        )
        new_high = jnp.maximum(highest, jnp.max(scores, axis=-1))
        shrink = jnp.exp(highest - new_high)
        weights = jnp.exp(scores - new_high[..., None])
        new_sum = weight_sum * shrink + jnp.sum(weights, axis=-1)
        probs = weights.astype(jnp.bfloat16)
        added = jnp.einsum("hqk,khd->hqd", probs, value_block, preferred_element_type=jnp.float32)
        return ((new_high, new_sum, weighted * shrink[..., None] + added), None)

    partial_value = lax.scan(advance, initial, (key_blocks, value_blocks))[0]
    weight_sum = partial_value[1]
    weighted = partial_value[2]
    result = weighted / weight_sum[..., None]
    outputs = result.transpose(1, 0, 2).reshape(half_rows, local_heads * HD).astype(jnp.bfloat16)
    return lax.all_to_all(outputs, "head", split_axis=0, concat_axis=1, tiled=True)


CHIP = ("seq", "head")
BF16 = jnp.bfloat16
F32 = jnp.float32
SWAP = [(0, 1), (1, 0)]


def inverse_rms(ref):
    widened = ref[...].astype(F32)
    return lax.rsqrt(jnp.mean(widened * widened, axis=-1, keepdims=True) + EPS)


def pack_kernel(groups, me_ref, *refs):
    sources, outs, (q_ref, k_ref, v_ref, qg_ref, kg_ref, sems) = refs[:5], refs[5:-6], refs[-6:]
    copies = [
        pltpu.make_async_copy(source, target, sems.at[place])
        for place, (source, target) in enumerate(zip(sources, refs[-6:-1]))
    ]
    for copy in copies:
        copy.start()
    for copy in copies:
        copy.wait()
    rows, width = q_ref.shape
    part = width // groups
    full_refs, far_refs = outs[:groups], outs[groups:]
    q_inverse, k_inverse = inverse_rms(q_ref), inverse_rms(k_ref)
    for step in range(groups):
        group = lax.bitwise_xor(me_ref[0], step)
        columns = pl.ds(pl.multiple_of(group * part, HD), part)
        v_part = v_ref[:, columns]
        k_part = (k_ref[:, columns].astype(F32) * k_inverse * kg_ref[:, columns]).astype(BF16)
        q_part = (q_ref[:, columns].astype(F32) * q_inverse * qg_ref[:, columns]).astype(BF16)
        full, far = full_refs[step], far_refs[step]
        far[0:rows, :] = v_part
        far[rows : 2 * rows, :] = k_part
        full[0:rows, :] = v_part
        full[rows : 2 * rows, :] = k_part
        full[2 * rows : 3 * rows, :] = q_part


def joined(refs, first, rows, columns):
    pieces = [ref[first : first + rows, columns].astype(F32) for ref in refs]
    return jnp.concatenate(pieces, axis=0).astype(BF16)


def head_scores(q_head, k_head):
    factor = 1.0 / math.sqrt(HD)
    dims = (((1,), (1,)), ((), ()))
    return lax.dot_general(q_head, k_head, dims, preferred_element_type=F32) * factor


def columns_of(head):
    return slice(head * HD, (head + 1) * HD)


def all_scores(query_refs, key_refs):
    rows, heads = query_refs[0].shape[0] // 3, query_refs[0].shape[1] // HD
    scores = []
    for head in range(heads):
        q_head = joined(query_refs, 2 * rows, rows, columns_of(head))
        scores.append(head_scores(q_head, joined(key_refs, rows, rows, columns_of(head))))
    return scores


def near_kernel(groups, *refs):
    near, (high_ref, sum_ref, acc_ref) = refs[:-3], refs[-3:]
    rows = near[0].shape[0] // 3
    all_weights = []
    for head, scores in enumerate(all_scores(near[:groups], near)):
        highest = jnp.max(scores, axis=-1, keepdims=True)
        weights = jnp.exp(scores - highest)
        high_ref[head] = jnp.broadcast_to(highest, high_ref.shape[1:])
        weight_sum = jnp.sum(weights, axis=-1, keepdims=True)
        sum_ref[head] = jnp.broadcast_to(weight_sum, sum_ref.shape[1:])
        all_weights.append(weights.astype(BF16))
    for head, weights in enumerate(all_weights):
        v_head = joined(near, 0, rows, columns_of(head))
        acc_ref[head] = jnp.dot(weights, v_head, preferred_element_type=F32)


def far_kernel(groups, high_ref, sum_ref, acc_ref, *refs):
    near, far, outs = refs[:groups], refs[groups : 3 * groups], refs[3 * groups :]
    rows = near[0].shape[0] // 3
    kept = []
    for head, scores in enumerate(all_scores(near, far)):
        before = high_ref[head]
        highest = jnp.maximum(before, jnp.max(scores, axis=-1, keepdims=True))
        weights = jnp.exp(scores - highest[:, 0:1])
        shrink = jnp.exp(before - highest)
        weight_sum = sum_ref[head] * shrink + jnp.sum(weights, axis=-1, keepdims=True)
        kept.append((weights.astype(BF16), acc_ref[head] * shrink, weight_sum))
    for head, (weights, acc, weight_sum) in enumerate(kept):
        v_head = joined(far, 0, rows, columns_of(head))
        added = jnp.dot(weights, v_head, preferred_element_type=F32)
        result = ((acc + added) / weight_sum).astype(BF16)
        for step in range(groups):
            outs[step][:, columns_of(head)] = result[step * rows : (step + 1) * rows, :]


def place_kernel(groups, me_ref, *refs):
    parts, out_ref = refs[:-1], refs[-1]
    part = parts[0].shape[1]
    for step in range(groups):
        group = lax.bitwise_xor(me_ref[0], step)
        out_ref[:, pl.ds(pl.multiple_of(group * part, HD), part)] = parts[step][...]


def kernel_call(kernel, shapes, scalars=0, fetched=(), scratch=(), limit=16 << 20):
    smem = pl.BlockSpec(memory_space=pltpu.SMEM)
    vmem = pl.BlockSpec(memory_space=pltpu.VMEM)
    hbm = pl.BlockSpec(memory_space=pltpu.HBM)

    def call(*args):
        places = [smem if i < scalars else hbm if i in fetched else vmem for i in range(len(args))]
        return pl.pallas_call(
            kernel,
            out_shape=shapes,
            in_specs=places,
            out_specs=jax.tree.map(lambda _: vmem, shapes),
            scratch_shapes=scratch,
            compiler_params=pltpu.CompilerParams(vmem_limit_bytes=limit),
        )(*args)

    return call


def halves_body(sizes, queries, keys, values, q_gain, k_gain):
    seq, across = sizes["seq"], sizes["head"]
    groups = seq // 2 * across
    rows, width = queries.shape
    part = width // groups
    heads = part // HD
    me = lax.axis_index("seq") % (seq // 2) * across + lax.axis_index("head")
    me = me.astype(jnp.int32).reshape(1)

    def send(value, half, step):
        place = half * (seq // 2) * across + step
        return lax.ppermute(value, CHIP, [(i, i ^ place) for i in range(seq * across)])

    def swap(value):
        return lax.ppermute(value, "sub", SWAP)

    steps = range(groups)
    full = jax.ShapeDtypeStruct((3 * rows, part), BF16)
    far = jax.ShapeDtypeStruct((2 * rows, part), BF16)
    token = pltpu.VMEM((rows, width), BF16)
    gain = pltpu.VMEM((1, width), F32)
    packed = kernel_call(
        functools.partial(pack_kernel, groups),
        [full] * groups + [far] * groups,
        scalars=1,
        fetched=range(1, 6),
        limit=60 << 20,
        scratch=[token] * 3 + [gain] * 2 + [pltpu.SemaphoreType.DMA((5,))],
    )(me, queries, keys, values, q_gain[None, :], k_gain[None, :])
    fulls, fars = packed[:groups], packed[groups:]
    far_in = [send(fars[step], 1, step) for step in steps]
    near_in = [fulls[0]] + [send(fulls[step], 0, step) for step in steps[1:]]
    near_other = [swap(near_in[step]) for step in steps]
    far_other = [swap(far_in[step]) for step in steps]
    state = jax.ShapeDtypeStruct((heads, groups * rows, HD), F32)
    partial = kernel_call(functools.partial(near_kernel, groups), [state] * 3)(
        *near_in, *near_other
    )
    piece = jax.ShapeDtypeStruct((rows, part), BF16)
    pieces = kernel_call(functools.partial(far_kernel, groups), [piece] * groups)(
        *partial, *near_in, *far_in, *far_other
    )
    back = [pieces[0]] + [send(pieces[step], 0, step) for step in steps[1:]]
    whole = jax.ShapeDtypeStruct((rows, width), BF16)
    return kernel_call(functools.partial(place_kernel, groups), whole, scalars=1)(me, *back)


def power_of_two(size):
    return size & (size - 1) == 0


def solution(mesh):
    sizes = mesh.shape
    groups = sizes["seq"] // 2 * sizes["head"]
    paired = sizes["sub"] == 2 and sizes["seq"] > 1
    paired = paired and power_of_two(sizes["seq"]) and power_of_two(sizes["head"])

    def body(queries, *rest):
        if paired and queries.shape[1] // HD % groups == 0:
            return halves_body(sizes, queries, *rest)
        return gathered_body(queries, *rest)

    token_spec = P(("grp", "seq", "head", "sub"), None)
    in_specs = (token_spec, token_spec, token_spec, P(), P())
    return jax.shard_map(
        body, mesh=mesh, in_specs=in_specs, out_specs=token_spec, check_vma=False
    )
```

```python
import functools
import math

import jax
import jax.numpy as jnp
from jax import lax
from jax.experimental import pallas as pl
from jax.experimental.pallas import tpu as pltpu
from jax.sharding import PartitionSpec as P


HD = 128


EPS = 1e-06


def normalize(matrix, gain):
    widened = matrix.astype(jnp.float32)
    inverse = lax.rsqrt(jnp.mean(widened * widened, axis=-1, keepdims=True) + EPS)
    return (widened * inverse * gain).astype(jnp.bfloat16)


def gathered_body(queries, keys, values, q_gain, k_gain):
    q_normed = normalize(queries, q_gain)
    k_normed = normalize(keys, k_gain)
    q_local, k_local, v_local = (
        lax.all_to_all(q_normed, "head", split_axis=1, concat_axis=0, tiled=True),
        lax.all_to_all(k_normed, "head", split_axis=1, concat_axis=0, tiled=True),
        lax.all_to_all(values, "head", split_axis=1, concat_axis=0, tiled=True),
    )
    query_count = q_local.shape[0]
    local_heads = q_local.shape[1] // HD
    factor = 1.0 / math.sqrt(HD)
    q_heads = q_local.reshape(query_count, local_heads, HD).transpose(1, 0, 2)
    initial = (
        jnp.full((local_heads, query_count), -1e30, jnp.float32),
        jnp.zeros((local_heads, query_count), jnp.float32),
        jnp.zeros((local_heads, query_count, HD), jnp.float32),
    )
    half_rows = q_local.shape[0]
    key_piece = lax.all_gather(k_local, ("seq", "sub"), axis=0, tiled=True)
    value_piece = lax.all_gather(v_local, ("seq", "sub"), axis=0, tiled=True)
    row_count = key_piece.shape[0]
    block_size = math.gcd(row_count, 512)
    turn_count = row_count // block_size
    key_blocks = key_piece.reshape(turn_count, block_size, local_heads, HD)
    value_blocks = value_piece.reshape(turn_count, block_size, local_heads, HD)

    def advance(state, block_pair):
        key_block, value_block = block_pair
        highest, weight_sum, weighted = state
        scores = (
            jnp.einsum("hqd,khd->hqk", q_heads, key_block, preferred_element_type=jnp.float32)
            * factor
        )
        new_high = jnp.maximum(highest, jnp.max(scores, axis=-1))
        shrink = jnp.exp(highest - new_high)
        weights = jnp.exp(scores - new_high[..., None])
        new_sum = weight_sum * shrink + jnp.sum(weights, axis=-1)
        probs = weights.astype(jnp.bfloat16)
        added = jnp.einsum("hqk,khd->hqd", probs, value_block, preferred_element_type=jnp.float32)
        return ((new_high, new_sum, weighted * shrink[..., None] + added), None)

    partial_value = lax.scan(advance, initial, (key_blocks, value_blocks))[0]
    weight_sum = partial_value[1]
    weighted = partial_value[2]
    result = weighted / weight_sum[..., None]
    outputs = result.transpose(1, 0, 2).reshape(half_rows, local_heads * HD).astype(jnp.bfloat16)
    return lax.all_to_all(outputs, "head", split_axis=0, concat_axis=1, tiled=True)


CHIP = ("seq", "head")
BF16 = jnp.bfloat16
F32 = jnp.float32
SWAP = [(0, 1), (1, 0)]


def inverse_rms(ref):
    widened = ref[...].astype(F32)
    return lax.rsqrt(jnp.mean(widened * widened, axis=-1, keepdims=True) + EPS)


def pack_kernel(groups, me_ref, *refs):
    sources, outs, (q_ref, k_ref, v_ref, qg_ref, kg_ref, sems) = refs[:5], refs[5:-6], refs[-6:]
    copies = [
        pltpu.make_async_copy(source, target, sems.at[place])
        for place, (source, target) in enumerate(zip(sources, refs[-6:-1]))
    ]
    for copy in copies:
        copy.start()
    for copy in copies:
        copy.wait()
    rows, width = q_ref.shape
    part = width // groups
    full_refs, far_refs = outs[:groups], outs[groups:]
    q_inverse, k_inverse = inverse_rms(q_ref), inverse_rms(k_ref)
    for step in range(groups):
        group = lax.bitwise_xor(me_ref[0], step)
        columns = pl.ds(pl.multiple_of(group * part, HD), part)
        v_part = v_ref[:, columns]
        k_part = (k_ref[:, columns].astype(F32) * k_inverse * kg_ref[:, columns]).astype(BF16)
        q_part = (q_ref[:, columns].astype(F32) * q_inverse * qg_ref[:, columns]).astype(BF16)
        full, far = full_refs[step], far_refs[step]
        far[0:rows, :] = v_part
        far[rows : 2 * rows, :] = k_part
        full[0:rows, :] = v_part
        full[rows : 2 * rows, :] = k_part
        full[2 * rows : 3 * rows, :] = q_part


def joined(refs, first, rows, columns):
    pieces = [ref[first : first + rows, columns].astype(F32) for ref in refs]
    return jnp.concatenate(pieces, axis=0).astype(BF16)


def head_scores(q_head, k_head):
    factor = 1.0 / math.sqrt(HD)
    dims = (((1,), (1,)), ((), ()))
    return lax.dot_general(q_head, k_head, dims, preferred_element_type=F32) * factor


def columns_of(head):
    return slice(head * HD, (head + 1) * HD)


def all_scores(query_refs, key_refs):
    rows, heads = query_refs[0].shape[0] // 3, query_refs[0].shape[1] // HD
    scores = []
    for head in range(heads):
        q_head = joined(query_refs, 2 * rows, rows, columns_of(head))
        scores.append(head_scores(q_head, joined(key_refs, rows, rows, columns_of(head))))
    return scores


def near_kernel(groups, *refs):
    near, (high_ref, sum_ref, acc_ref) = refs[:-3], refs[-3:]
    rows = near[0].shape[0] // 3
    all_weights = []
    for head, scores in enumerate(all_scores(near[:groups], near)):
        highest = jnp.max(scores, axis=-1, keepdims=True)
        weights = jnp.exp(scores - highest)
        high_ref[head] = jnp.broadcast_to(highest, high_ref.shape[1:])
        weight_sum = jnp.sum(weights, axis=-1, keepdims=True)
        sum_ref[head] = jnp.broadcast_to(weight_sum, sum_ref.shape[1:])
        all_weights.append(weights.astype(BF16))
    for head, weights in enumerate(all_weights):
        v_head = joined(near, 0, rows, columns_of(head))
        acc_ref[head] = jnp.dot(weights, v_head, preferred_element_type=F32)


def far_kernel(groups, high_ref, sum_ref, acc_ref, *refs):
    near, far, outs = refs[:groups], refs[groups : 3 * groups], refs[3 * groups :]
    rows = near[0].shape[0] // 3
    kept = []
    for head, scores in enumerate(all_scores(near, far)):
        before = high_ref[head]
        highest = jnp.maximum(before, jnp.max(scores, axis=-1, keepdims=True))
        weights = jnp.exp(scores - highest[:, 0:1])
        shrink = jnp.exp(before - highest)
        weight_sum = sum_ref[head] * shrink + jnp.sum(weights, axis=-1, keepdims=True)
        kept.append((weights.astype(BF16), acc_ref[head] * shrink, weight_sum))
    for head, (weights, acc, weight_sum) in enumerate(kept):
        v_head = joined(far, 0, rows, columns_of(head))
        added = jnp.dot(weights, v_head, preferred_element_type=F32)
        result = ((acc + added) / weight_sum).astype(BF16)
        for step in range(groups):
            outs[step][:, columns_of(head)] = result[step * rows : (step + 1) * rows, :]


def place_kernel(groups, me_ref, *refs):
    parts, out_ref = refs[:-1], refs[-1]
    part = parts[0].shape[1]
    for step in range(groups):
        group = lax.bitwise_xor(me_ref[0], step)
        out_ref[:, pl.ds(pl.multiple_of(group * part, HD), part)] = parts[step][...]


def kernel_call(kernel, shapes, scalars=0, fetched=(), scratch=(), limit=16 << 20):
    smem = pl.BlockSpec(memory_space=pltpu.SMEM)
    vmem = pl.BlockSpec(memory_space=pltpu.VMEM)
    hbm = pl.BlockSpec(memory_space=pltpu.HBM)

    def call(*args):
        places = [smem if i < scalars else hbm if i in fetched else vmem for i in range(len(args))]
        return pl.pallas_call(
            kernel,
            out_shape=shapes,
            in_specs=places,
            out_specs=jax.tree.map(lambda _: vmem, shapes),
            scratch_shapes=scratch,
            compiler_params=pltpu.CompilerParams(vmem_limit_bytes=limit),
        )(*args)

    return call


def halves_body(sizes, queries, keys, values, q_gain, k_gain):
    seq, across = sizes["seq"], sizes["head"]
    groups = seq // 2 * across
    rows, width = queries.shape
    part = width // groups
    heads = part // HD
    me = lax.axis_index("seq") % (seq // 2) * across + lax.axis_index("head")
    me = me.astype(jnp.int32).reshape(1)

    def send(value, half, step):
        place = half * (seq // 2) * across + step
        return lax.ppermute(value, CHIP, [(i, i ^ place) for i in range(seq * across)])

    def swap(value):
        return lax.ppermute(value, "sub", SWAP)

    steps = range(groups)
    full = jax.ShapeDtypeStruct((3 * rows, part), BF16)
    far = jax.ShapeDtypeStruct((2 * rows, part), BF16)
    token = pltpu.VMEM((rows, width), BF16)
    gain = pltpu.VMEM((1, width), F32)
    held = [
        pltpu.with_memory_space_constraint(value, pltpu.HBM)
        for value in (queries, keys, values, q_gain[None, :], k_gain[None, :])
    ]
    packed = kernel_call(
        functools.partial(pack_kernel, groups),
        [full] * groups + [far] * groups,
        scalars=1,
        fetched=range(1, 6),
        scratch=[token] * 3 + [gain] * 2 + [pltpu.SemaphoreType.DMA((5,))],
    )(me, *held)
    fulls, fars = packed[:groups], packed[groups:]
    far_in = [send(fars[step], 1, step) for step in steps]
    near_in = [fulls[0]] + [send(fulls[step], 0, step) for step in steps[1:]]
    near_other = [swap(near_in[step]) for step in steps]
    far_other = [swap(far_in[step]) for step in steps]
    state = jax.ShapeDtypeStruct((heads, groups * rows, HD), F32)
    partial = kernel_call(functools.partial(near_kernel, groups), [state] * 3)(
        *near_in, *near_other
    )
    piece = jax.ShapeDtypeStruct((rows, part), BF16)
    pieces = kernel_call(functools.partial(far_kernel, groups), [piece] * groups)(
        *partial, *near_in, *far_in, *far_other
    )
    back = [pieces[0]] + [send(pieces[step], 0, step) for step in steps[1:]]
    whole = jax.ShapeDtypeStruct((rows, width), BF16)
    return kernel_call(functools.partial(place_kernel, groups), whole, scalars=1)(me, *back)


def power_of_two(size):
    return size & (size - 1) == 0


def solution(mesh):
    sizes = mesh.shape
    groups = sizes["seq"] // 2 * sizes["head"]
    paired = sizes["sub"] == 2 and sizes["seq"] > 1
    paired = paired and power_of_two(sizes["seq"]) and power_of_two(sizes["head"])

    def body(queries, *rest):
        if paired and queries.shape[1] // HD % groups == 0:
            return halves_body(sizes, queries, *rest)
        return gathered_body(queries, *rest)

    token_spec = P(("grp", "seq", "head", "sub"), None)
    in_specs = (token_spec, token_spec, token_spec, P(), P())
    return jax.shard_map(
        body, mesh=mesh, in_specs=in_specs, out_specs=token_spec, check_vma=False
    )
```

```python
import functools
import math

import jax
import jax.numpy as jnp
from jax import lax
from jax.experimental import pallas as pl
from jax.experimental.pallas import tpu as pltpu
from jax.sharding import PartitionSpec as P


HD = 128


EPS = 1e-06


def normalize(matrix, gain):
    widened = matrix.astype(jnp.float32)
    inverse = lax.rsqrt(jnp.mean(widened * widened, axis=-1, keepdims=True) + EPS)
    return (widened * inverse * gain).astype(jnp.bfloat16)


def gathered_body(queries, keys, values, q_gain, k_gain):
    q_normed = normalize(queries, q_gain)
    k_normed = normalize(keys, k_gain)
    q_local, k_local, v_local = (
        lax.all_to_all(q_normed, "head", split_axis=1, concat_axis=0, tiled=True),
        lax.all_to_all(k_normed, "head", split_axis=1, concat_axis=0, tiled=True),
        lax.all_to_all(values, "head", split_axis=1, concat_axis=0, tiled=True),
    )
    query_count = q_local.shape[0]
    local_heads = q_local.shape[1] // HD
    factor = 1.0 / math.sqrt(HD)
    q_heads = q_local.reshape(query_count, local_heads, HD).transpose(1, 0, 2)
    initial = (
        jnp.full((local_heads, query_count), -1e30, jnp.float32),
        jnp.zeros((local_heads, query_count), jnp.float32),
        jnp.zeros((local_heads, query_count, HD), jnp.float32),
    )
    half_rows = q_local.shape[0]
    key_piece = lax.all_gather(k_local, ("seq", "sub"), axis=0, tiled=True)
    value_piece = lax.all_gather(v_local, ("seq", "sub"), axis=0, tiled=True)
    row_count = key_piece.shape[0]
    block_size = math.gcd(row_count, 512)
    turn_count = row_count // block_size
    key_blocks = key_piece.reshape(turn_count, block_size, local_heads, HD)
    value_blocks = value_piece.reshape(turn_count, block_size, local_heads, HD)

    def advance(state, block_pair):
        key_block, value_block = block_pair
        highest, weight_sum, weighted = state
        scores = (
            jnp.einsum("hqd,khd->hqk", q_heads, key_block, preferred_element_type=jnp.float32)
            * factor
        )
        new_high = jnp.maximum(highest, jnp.max(scores, axis=-1))
        shrink = jnp.exp(highest - new_high)
        weights = jnp.exp(scores - new_high[..., None])
        new_sum = weight_sum * shrink + jnp.sum(weights, axis=-1)
        probs = weights.astype(jnp.bfloat16)
        added = jnp.einsum("hqk,khd->hqd", probs, value_block, preferred_element_type=jnp.float32)
        return ((new_high, new_sum, weighted * shrink[..., None] + added), None)

    partial_value = lax.scan(advance, initial, (key_blocks, value_blocks))[0]
    weight_sum = partial_value[1]
    weighted = partial_value[2]
    result = weighted / weight_sum[..., None]
    outputs = result.transpose(1, 0, 2).reshape(half_rows, local_heads * HD).astype(jnp.bfloat16)
    return lax.all_to_all(outputs, "head", split_axis=0, concat_axis=1, tiled=True)


BF16 = jnp.bfloat16
F32 = jnp.float32
SWAP = [(0, 1), (1, 0)]


def inverse_rms(ref):
    widened = ref[...].astype(F32)
    return lax.rsqrt(jnp.mean(widened * widened, axis=-1, keepdims=True) + EPS)


def pack_kernel(groups, me_ref, *refs):
    sources, outs, (q_ref, k_ref, v_ref, qg_ref, kg_ref, sems) = refs[:5], refs[5:-6], refs[-6:]
    copies = [
        pltpu.make_async_copy(source, target, sems.at[place])
        for place, (source, target) in enumerate(zip(sources, refs[-6:-1]))
    ]
    for copy in copies:
        copy.start()
    for copy in copies:
        copy.wait()
    rows, width = q_ref.shape
    part = width // groups
    pair_refs, query_refs = outs[:groups], outs[groups:]
    q_inverse, k_inverse = inverse_rms(q_ref), inverse_rms(k_ref)
    for step in range(groups):
        group = lax.bitwise_xor(me_ref[0], step)
        columns = pl.ds(pl.multiple_of(group * part, HD), part)
        k_part = k_ref[:, columns].astype(F32) * k_inverse * kg_ref[:, columns]
        q_part = q_ref[:, columns].astype(F32) * q_inverse * qg_ref[:, columns]
        pair_refs[step][0:rows, :] = v_ref[:, columns]
        pair_refs[step][rows : 2 * rows, :] = k_part.astype(BF16)
        query_refs[step][...] = q_part.astype(BF16)


def joined(refs, first, rows, columns):
    pieces = [ref[first : first + rows, columns].astype(F32) for ref in refs]
    return jnp.concatenate(pieces, axis=0).astype(BF16)


def columns_of(head):
    return slice(head * HD, (head + 1) * HD)


def attend_kernel(groups, *refs):
    queries, pairs, outs = refs[:groups], refs[groups:-groups], refs[-groups:]
    rows, width = queries[0].shape
    factor = 1.0 / math.sqrt(HD)
    dims = (((1,), (1,)), ((), ()))
    heads = range(width // HD)
    all_scores = []
    for head in heads:
        q_head = joined(queries, 0, rows, columns_of(head))
        k_head = joined(pairs, rows, rows, columns_of(head))
        scores = lax.dot_general(q_head, k_head, dims, preferred_element_type=F32)
        all_scores.append(scores * factor)
    kept = []
    for scores in all_scores:
        highest = jnp.max(scores, axis=-1, keepdims=True)
        weights = jnp.exp(scores - highest)
        kept.append((weights.astype(BF16), jnp.sum(weights, axis=-1, keepdims=True)))
    for head, (weights, weight_sum) in zip(heads, kept):
        v_head = joined(pairs, 0, rows, columns_of(head))
        weighted = jnp.dot(weights, v_head, preferred_element_type=F32)
        result = (weighted / weight_sum).astype(BF16)
        for step in range(groups):
            outs[step][:, columns_of(head)] = result[step * rows : (step + 1) * rows, :]


def place_kernel(groups, me_ref, *refs):
    parts, out_ref = refs[:-1], refs[-1]
    part = parts[0].shape[1]
    for step in range(groups):
        group = lax.bitwise_xor(me_ref[0], step)
        out_ref[:, pl.ds(pl.multiple_of(group * part, HD), part)] = parts[step][...]


def kernel_call(kernel, shapes, scalars=0, fetched=(), scratch=(), limit=16 << 20):
    smem = pl.BlockSpec(memory_space=pltpu.SMEM)
    vmem = pl.BlockSpec(memory_space=pltpu.VMEM)
    hbm = pl.BlockSpec(memory_space=pltpu.HBM)

    def call(*args):
        places = [smem if i < scalars else hbm if i in fetched else vmem for i in range(len(args))]
        return pl.pallas_call(
            kernel,
            out_shape=shapes,
            in_specs=places,
            out_specs=jax.tree.map(lambda _: vmem, shapes),
            scratch_shapes=scratch,
            compiler_params=pltpu.CompilerParams(vmem_limit_bytes=limit),
        )(*args)

    return call


def columns_body(groups, queries, keys, values, q_gain, k_gain):
    rows, width = queries.shape
    part = width // groups
    me = lax.axis_index("seq").astype(jnp.int32).reshape(1)
    steps = range(groups)

    def send(value, step):
        return lax.ppermute(value, "seq", [(i, i ^ step) for i in steps])

    def swap(axis, value):
        return lax.ppermute(value, axis, SWAP)

    pair = jax.ShapeDtypeStruct((2 * rows, part), BF16)
    piece = jax.ShapeDtypeStruct((rows, part), BF16)
    token = pltpu.VMEM((rows, width), BF16)
    gain = pltpu.VMEM((1, width), F32)
    held = [
        pltpu.with_memory_space_constraint(value, pltpu.HBM)
        for value in (queries, keys, values, q_gain[None, :], k_gain[None, :])
    ]
    packed = kernel_call(
        functools.partial(pack_kernel, groups),
        [pair] * groups + [piece] * groups,
        scalars=1,
        fetched=range(1, 6),
        scratch=[token] * 3 + [gain] * 2 + [pltpu.SemaphoreType.DMA((5,))],
    )(me, *held)
    pairs, asked = packed[:groups], packed[groups:]
    mine = [pairs[0]] + [send(pairs[step], step) for step in steps[1:]]
    asked = [asked[0]] + [send(asked[step], step) for step in steps[1:]]
    beside = [swap("head", mine[step]) for step in steps]
    blocks = mine + beside
    blocks += [swap("sub", mine[step]) for step in steps]
    blocks += [swap("sub", beside[step]) for step in steps]
    pieces = kernel_call(functools.partial(attend_kernel, groups), [piece] * groups)(
        *asked, *blocks
    )
    back = [pieces[0]] + [send(pieces[step], step) for step in steps[1:]]
    whole = jax.ShapeDtypeStruct((rows, width), BF16)
    return kernel_call(functools.partial(place_kernel, groups), whole, scalars=1)(me, *back)


def power_of_two(size):
    return size & (size - 1) == 0


def solution(mesh):
    sizes = mesh.shape
    groups = sizes["seq"]
    paired = sizes["sub"] == 2 and sizes["head"] == 2 and power_of_two(groups)

    def body(queries, *rest):
        if paired and queries.shape[1] // HD % groups == 0:
            return columns_body(groups, queries, *rest)
        return gathered_body(queries, *rest)

    token_spec = P(("grp", "seq", "head", "sub"), None)
    in_specs = (token_spec, token_spec, token_spec, P(), P())
    return jax.shard_map(
        body, mesh=mesh, in_specs=in_specs, out_specs=token_spec, check_vma=False
    )
```

```python
import functools
import math

import jax
import jax.numpy as jnp
from jax import lax
from jax.experimental import pallas as pl
from jax.experimental.pallas import tpu as pltpu
from jax.sharding import PartitionSpec as P


HD = 128


EPS = 1e-06


def normalize(matrix, gain):
    widened = matrix.astype(jnp.float32)
    inverse = lax.rsqrt(jnp.mean(widened * widened, axis=-1, keepdims=True) + EPS)
    return (widened * inverse * gain).astype(jnp.bfloat16)


def gathered_body(queries, keys, values, q_gain, k_gain):
    q_normed = normalize(queries, q_gain)
    k_normed = normalize(keys, k_gain)
    q_local, k_local, v_local = (
        lax.all_to_all(q_normed, "head", split_axis=1, concat_axis=0, tiled=True),
        lax.all_to_all(k_normed, "head", split_axis=1, concat_axis=0, tiled=True),
        lax.all_to_all(values, "head", split_axis=1, concat_axis=0, tiled=True),
    )
    query_count = q_local.shape[0]
    local_heads = q_local.shape[1] // HD
    factor = 1.0 / math.sqrt(HD)
    q_heads = q_local.reshape(query_count, local_heads, HD).transpose(1, 0, 2)
    initial = (
        jnp.full((local_heads, query_count), -1e30, jnp.float32),
        jnp.zeros((local_heads, query_count), jnp.float32),
        jnp.zeros((local_heads, query_count, HD), jnp.float32),
    )
    half_rows = q_local.shape[0]
    key_piece = lax.all_gather(k_local, ("seq", "sub"), axis=0, tiled=True)
    value_piece = lax.all_gather(v_local, ("seq", "sub"), axis=0, tiled=True)
    row_count = key_piece.shape[0]
    block_size = math.gcd(row_count, 512)
    turn_count = row_count // block_size
    key_blocks = key_piece.reshape(turn_count, block_size, local_heads, HD)
    value_blocks = value_piece.reshape(turn_count, block_size, local_heads, HD)

    def advance(state, block_pair):
        key_block, value_block = block_pair
        highest, weight_sum, weighted = state
        scores = (
            jnp.einsum("hqd,khd->hqk", q_heads, key_block, preferred_element_type=jnp.float32)
            * factor
        )
        new_high = jnp.maximum(highest, jnp.max(scores, axis=-1))
        shrink = jnp.exp(highest - new_high)
        weights = jnp.exp(scores - new_high[..., None])
        new_sum = weight_sum * shrink + jnp.sum(weights, axis=-1)
        probs = weights.astype(jnp.bfloat16)
        added = jnp.einsum("hqk,khd->hqd", probs, value_block, preferred_element_type=jnp.float32)
        return ((new_high, new_sum, weighted * shrink[..., None] + added), None)

    partial_value = lax.scan(advance, initial, (key_blocks, value_blocks))[0]
    weight_sum = partial_value[1]
    weighted = partial_value[2]
    result = weighted / weight_sum[..., None]
    outputs = result.transpose(1, 0, 2).reshape(half_rows, local_heads * HD).astype(jnp.bfloat16)
    return lax.all_to_all(outputs, "head", split_axis=0, concat_axis=1, tiled=True)


BF16 = jnp.bfloat16
F32 = jnp.float32
SWAP = [(0, 1), (1, 0)]


def inverse_rms(ref):
    widened = ref[...].astype(F32)
    return lax.rsqrt(jnp.mean(widened * widened, axis=-1, keepdims=True) + EPS)


def pack_kernel(groups, joint, me_ref, *refs):
    sources, outs, (q_ref, k_ref, v_ref, qg_ref, kg_ref, sems) = refs[:5], refs[5:-6], refs[-6:]
    copies = [
        pltpu.make_async_copy(source, target, sems.at[place])
        for place, (source, target) in enumerate(zip(sources, refs[-6:-1]))
    ]
    for copy in copies:
        copy.start()
    for copy in copies:
        copy.wait()
    rows, width = q_ref.shape
    part = width // groups
    outs = list(outs)
    q_inverse, k_inverse = inverse_rms(q_ref), inverse_rms(k_ref)
    for step in range(groups):
        group = lax.bitwise_xor(me_ref[0], step)
        columns = pl.ds(pl.multiple_of(group * part, HD), part)
        k_part = k_ref[:, columns].astype(F32) * k_inverse * kg_ref[:, columns]
        q_part = q_ref[:, columns].astype(F32) * q_inverse * qg_ref[:, columns]
        pair = outs.pop(0)
        pair[0:rows, :] = v_ref[:, columns]
        pair[rows : 2 * rows, :] = k_part.astype(BF16)
        if step in joint:
            pair[2 * rows : 3 * rows, :] = q_part.astype(BF16)
        else:
            outs.pop(0)[...] = q_part.astype(BF16)


def joined(refs, first, rows, stride, columns):
    pieces = [
        ref[start : start + rows, columns].astype(F32)
        for ref in refs
        for start in range(first % ref.shape[0], ref.shape[0] // stride * stride, stride)
    ]
    return jnp.concatenate(pieces, axis=0).astype(BF16)


def queried(refs, rows, columns):
    pieces = [ref[ref.shape[0] - rows : ref.shape[0], columns].astype(F32) for ref in refs]
    return jnp.concatenate(pieces, axis=0).astype(BF16)


def columns_of(head):
    return slice(head * HD, (head + 1) * HD)


def attend_kernel(groups, *refs):
    queries, pairs, outs = refs[:groups], refs[groups:-groups], refs[-groups:]
    rows, width = outs[0].shape
    factor = 1.0 / math.sqrt(HD)
    dims = (((1,), (1,)), ((), ()))
    heads = range(width // HD)
    all_scores = []
    for head in heads:
        q_head = queried(queries, rows, columns_of(head))
        k_head = joined(pairs, rows, rows, 2 * rows, columns_of(head))
        scores = lax.dot_general(q_head, k_head, dims, preferred_element_type=F32)
        all_scores.append(scores * factor)
    kept = []
    for scores in all_scores:
        highest = jnp.max(scores, axis=-1, keepdims=True)
        weights = jnp.exp(scores - highest)
        kept.append((weights.astype(BF16), jnp.sum(weights, axis=-1, keepdims=True)))
    for head, (weights, weight_sum) in zip(heads, kept):
        v_head = joined(pairs, 0, rows, 2 * rows, columns_of(head))
        weighted = jnp.dot(weights, v_head, preferred_element_type=F32)
        result = (weighted / weight_sum).astype(BF16)
        for step in range(groups):
            outs[step][:, columns_of(head)] = result[step * rows : (step + 1) * rows, :]


def place_kernel(groups, me_ref, *refs):
    parts, out_ref = refs[:-1], refs[-1]
    part = parts[0].shape[1]
    for step in range(groups):
        group = lax.bitwise_xor(me_ref[0], step)
        out_ref[:, pl.ds(pl.multiple_of(group * part, HD), part)] = parts[step][...]


def kernel_call(kernel, shapes, scalars=0, fetched=(), scratch=(), limit=16 << 20):
    smem = pl.BlockSpec(memory_space=pltpu.SMEM)
    vmem = pl.BlockSpec(memory_space=pltpu.VMEM)
    hbm = pl.BlockSpec(memory_space=pltpu.HBM)

    def call(*args):
        places = [smem if i < scalars else hbm if i in fetched else vmem for i in range(len(args))]
        return pl.pallas_call(
            kernel,
            out_shape=shapes,
            in_specs=places,
            out_specs=jax.tree.map(lambda _: vmem, shapes),
            scratch_shapes=scratch,
            compiler_params=pltpu.CompilerParams(vmem_limit_bytes=limit),
        )(*args)

    return call


def columns_body(groups, queries, keys, values, q_gain, k_gain):
    rows, width = queries.shape
    part = width // groups
    me = lax.axis_index("seq").astype(jnp.int32).reshape(1)
    steps = range(groups)

    def send(value, step):
        return lax.ppermute(value, "seq", [(i, i ^ step) for i in steps])

    def swap(axis, value):
        return lax.ppermute(value, axis, SWAP)

    pair = jax.ShapeDtypeStruct((2 * rows, part), BF16)
    piece = jax.ShapeDtypeStruct((rows, part), BF16)
    token = pltpu.VMEM((rows, width), BF16)
    gain = pltpu.VMEM((1, width), F32)
    held = [
        pltpu.with_memory_space_constraint(value, pltpu.HBM)
        for value in (queries, keys, values, q_gain[None, :], k_gain[None, :])
    ]
    joint = steps[1:2]
    triple = jax.ShapeDtypeStruct((3 * rows, part), BF16)
    shapes = [shape for step in steps for shape in ([triple] if step in joint else [pair, piece])]
    packed = kernel_call(
        functools.partial(pack_kernel, groups, joint),
        shapes,
        scalars=1,
        fetched=range(1, 6),
        scratch=[token] * 3 + [gain] * 2 + [pltpu.SemaphoreType.DMA((5,))],
    )(me, *held)
    packed = list(packed)
    mine, sent, asked = [], [], []
    for step in steps:
        chunk = packed.pop(0)
        chunk = send(chunk, step) if step else chunk
        mine.append(chunk)
        sent.append(chunk[: 2 * rows])
        if step in joint:
            asked.append(chunk)
        else:
            query = packed.pop(0)
            asked.append(send(query, step) if step else query)
    beside = [swap("head", sent[step]) for step in steps]
    blocks = mine + beside
    for early in [steps[:-1]]:
        held = [block for step in early for block in (sent[step], beside[step])]
        blocks.append(swap("sub", jnp.concatenate(held, axis=0)))
    blocks.append(swap("sub", sent[-1]))
    blocks.append(swap("sub", beside[-1]))
    pieces = kernel_call(functools.partial(attend_kernel, groups), [piece] * groups)(
        *asked, *blocks
    )
    back = [pieces[0]] + [send(pieces[step], step) for step in steps[1:]]
    whole = jax.ShapeDtypeStruct((rows, width), BF16)
    return kernel_call(functools.partial(place_kernel, groups), whole, scalars=1)(me, *back)


def power_of_two(size):
    return size & (size - 1) == 0


def solution(mesh):
    sizes = mesh.shape
    groups = sizes["seq"]
    paired = sizes["sub"] == 2 and sizes["head"] == 2 and power_of_two(groups)

    def body(queries, *rest):
        if paired and queries.shape[1] // HD % groups == 0:
            return columns_body(groups, queries, *rest)
        return gathered_body(queries, *rest)

    token_spec = P(("grp", "seq", "head", "sub"), None)
    in_specs = (token_spec, token_spec, token_spec, P(), P())
    return jax.shard_map(
        body, mesh=mesh, in_specs=in_specs, out_specs=token_spec, check_vma=False
    )
```
